256 devices in a mesh: lat: 4 (over y_lo, core), lon: 16 (over y_hi, z), ch: 4 (over x).
Axes of the slice: x: 4, y: 4 (y_hi: 2, y_lo: 2; y = y_hi * 2 + y_lo), z: 8, core: 2. Of those that a mesh axis runs over, the one named last changes fastest.
Arguments:
- grid_field: bfloat16 [1440, 4, 49152], P('lon', 'ch', 'lat'), may hold values from -6 to 6
- first_weight: bfloat16 [4, 2, 96, 96], P('ch'), may hold values from -0.4375 to 0.4375
- first_bias: float32 [4, 2, 96], P('ch'), may hold values from -3 to 3
- second_weight: bfloat16 [4, 2, 96, 96], P('ch'), may hold values from -0.4375 to 0.4375
- second_bias: float32 [4, 2, 96], P('ch'), may hold values from -3 to 3
Outputs:
- mixed: bfloat16 [1440, 4, 49152], P('lon', 'ch', 'lat')
The draws below stay inside these ranges and needn't reach their ends.
All inputs are finite; a program needn't handle non-finite values.
Results may differ from the reference program's by a relative error of at most 0.0073.
Values may be sent and summed in bfloat16 or wider, within the bound.
No kernel may reach another device: no remote copies, remote signals or barrier semaphores. Data moves between devices by JAX's collectives and lax.ppermute only.
A program may use at most 128 MiB of HBM per device.

```python
import math
import jax
import jax.numpy as jnp
from jax import lax

H = 512
W = 1440
NB = 4
CB = 96


def level_of(stream_key, extent, pieces, least, high):
    level, own = 1.0, jax.random.fold_in(stream_key, 6)
    for dim, parts in pieces:
        steps = jnp.exp(jax.random.uniform(jax.random.fold_in(own, dim), (parts,), jnp.float32, least / len(pieces), high / len(pieces)))
        level = level * jnp.repeat(steps, extent[dim] // parts).reshape([-1 if axis == dim else 1 for axis in range(len(extent))])
    return level


def scatter_about(key, shape, spread, most, cuts=(), kind=jnp.bfloat16):
    gain = level_of(key, shape, cuts, -0.22, 0.18) if cuts else 1.0
    drawn = jax.random.normal(key, shape, jnp.float32) * spread * gain
    return jnp.minimum(jnp.maximum(drawn, -most), most).astype(kind)


def setup_inputs(seed: int = 0) -> dict:
    streams_of = jax.random.split(jax.random.key(seed), 6)
    return {
        "grid_field": scatter_about(streams_of[0], (W, NB, H * CB), 1.0, 6.0, ((0, 16), (1, 4), (2, 4))),
        "first_weight": scatter_about(streams_of[1], (NB, 2, CB, CB), (2 * CB) ** -0.5, 0.4375, ((0, 4),)),
        "first_bias": scatter_about(streams_of[2], (NB, 2, CB), 0.5, 3.0, ((0, 4),), jnp.float32),
        "second_weight": scatter_about(streams_of[3], (NB, 2, CB, CB), (2 * CB) ** -0.5, 0.4375, ((0, 4),)),
        "second_bias": scatter_about(streams_of[4], (NB, 2, CB), 0.5, 3.0, ((0, 4),), jnp.float32),
    }


shrink_level = 0.01

def phase_tables(length):
    indices = jnp.arange(length, dtype=jnp.int32)
    product = indices[:, None] * indices[None, :] % length
    angles = product.astype(jnp.float32) * (2.0 * math.pi / length)
    return (jnp.cos(angles), jnp.sin(angles))

def lon_tables(length):
    cosine_tab, sine_tab = phase_tables(length)
    kept_modes = length // 2
    factor = 1.0 / math.sqrt(length)
    forward = jnp.concatenate([cosine_tab[:kept_modes], -sine_tab[:kept_modes]], axis=0) * factor
    weights = jnp.where(jnp.arange(kept_modes) == 0, 1.0, 2.0).astype(jnp.float32)
    inverse = jnp.concatenate([cosine_tab[:, :kept_modes] * weights, -sine_tab[:, :kept_modes] * weights], axis=1) * factor
    return (forward.astype(jnp.bfloat16), inverse.astype(jnp.bfloat16))

def lat_tables(length):
    cosine_tab, sine_tab = phase_tables(length)
    factor = 1.0 / math.sqrt(length)
    forward = jnp.stack([jnp.stack([cosine_tab, sine_tab], axis=1), jnp.stack([-sine_tab, cosine_tab], axis=1)], axis=0) * factor
    inverse = jnp.stack([jnp.stack([cosine_tab, -sine_tab], axis=1), jnp.stack([sine_tab, cosine_tab], axis=1)], axis=0) * factor
    return (forward.astype(jnp.bfloat16), inverse.astype(jnp.bfloat16))

def complex_weight(weight):
    real_part, imag_part = (weight[0], weight[1])
    return jnp.stack([jnp.stack([real_part, imag_part], axis=1), jnp.stack([-imag_part, real_part], axis=1)], axis=0)

def block_mixing(mode_data, weight_one, bias_one, weight_two, bias_two):
    hidden = jnp.einsum('rkqc,rcsd->skqd', mode_data.astype(jnp.float32), complex_weight(weight_one).astype(jnp.float32), precision=lax.Precision.HIGHEST)
    hidden = jax.nn.relu(hidden + bias_one[:, None, None, :]).astype(jnp.bfloat16)
    output = jnp.einsum('rkqc,rcsd->skqd', hidden.astype(jnp.float32), complex_weight(weight_two).astype(jnp.float32), precision=lax.Precision.HIGHEST)
    output = output + bias_two[:, None, None, :]
    shrunk = jnp.sign(output) * jnp.maximum(jnp.abs(output) - shrink_level, 0.0)
    return shrunk.astype(jnp.bfloat16)

def reference(grid_field, first_weight, first_bias, second_weight, second_bias):
    kept_modes = W // 2
    lon_forward, lon_inverse = lon_tables(W)
    lat_forward, lat_inverse = lat_tables(H)
    lat_forward32 = lat_forward.astype(jnp.float32)
    lat_inverse32 = lat_inverse.astype(jnp.float32)
    blocks = jnp.moveaxis(grid_field, 1, 0)

    def per_block(inputs):
        block_field, weight_one, bias_one, weight_two, bias_two = inputs
        columns = block_field.reshape(W, H * CB)
        spectra = jnp.dot(lon_forward, columns, preferred_element_type=jnp.float32).astype(jnp.bfloat16)
        spectra = spectra.reshape(2, kept_modes, H, CB)
        mode_data = jnp.einsum('sqrh,rkhc->skqc', lat_forward32, spectra.astype(jnp.float32), precision=lax.Precision.HIGHEST).astype(jnp.bfloat16)
        shrunk = block_mixing(mode_data, weight_one, bias_one, weight_two, bias_two)
        returned = jnp.einsum('sqrh,rkhc->skqc', lat_inverse32, shrunk.astype(jnp.float32), precision=lax.Precision.HIGHEST).astype(jnp.bfloat16)
        grid_out = jnp.dot(lon_inverse, returned.reshape(2 * kept_modes, H * CB), preferred_element_type=jnp.float32) + columns.astype(jnp.float32)
        return grid_out.astype(jnp.bfloat16)
    mixed = lax.map(per_block, (blocks, first_weight, first_bias, second_weight, second_bias))
    return jnp.moveaxis(mixed, 0, 1)
```

```python
import functools
import math

import jax
import jax.numpy as jnp
import numpy as np
from jax import lax
from jax.experimental import pallas as pl
from jax.experimental.pallas import tpu as pltpu
from jax.sharding import PartitionSpec as P

shrink_level = 0.01
group = ("lat", "lon")


def phases(left, right, length):
    product = (left[:, None].astype(np.int64) * right[None, :]) % length
    angles = product.astype(np.float32) * np.float32(2.0 * math.pi / length)
    angles = angles.astype(np.float64)
    return np.cos(angles).astype(np.float32), np.sin(angles).astype(np.float32)


def lon_tables(lat_devices, lon_devices, local_lon, rows):
    length = local_lon * lon_devices
    kept = length // 2
    i, j, r = np.meshgrid(
        np.arange(lat_devices), np.arange(lon_devices), np.arange(rows), indexing="ij"
    )
    offset = (i * rows + r).reshape(-1)
    place = (j.reshape(-1) * local_lon + offset).astype(np.int64)
    real = (offset < local_lon).astype(np.float32)
    place = np.where(offset < local_lon, place, 0)
    cosine, sine = phases(np.arange(kept), place, length)
    factor = np.float32(1.0 / math.sqrt(length))
    forward = np.concatenate([cosine, -sine], axis=0) * factor * real
    weights = np.where(np.arange(kept) == 0, 1.0, 2.0).astype(np.float32)[:, None]
    inverse = np.concatenate([cosine * weights, -sine * weights], axis=0).T * factor
    inverse = inverse * real[:, None]
    return forward.astype(jnp.bfloat16), inverse.astype(jnp.bfloat16)


def lat_table(length):
    half = length // 2
    cosine, sine = phases(np.arange(half + 1), np.arange(length), length)
    sine[0] = cosine[half]
    table = np.stack([cosine[:half], sine[:half]], axis=1).reshape(length, length)
    return (table * np.float32(1.0 / math.sqrt(length))).astype(jnp.bfloat16)


def first_layer(weight, special):
    u, v = weight[0], weight[1]
    z = jnp.zeros_like(u)
    rows = lambda *blocks: jnp.concatenate([jnp.concatenate(b, axis=1) for b in blocks], axis=0)
    pair = rows((u, v, u, v), (v, -u, -v, u), (-v, u, -v, u), (u, v, -u, -v))
    single = rows((u, v, z, z), (z, z, u, v), (-v, u, z, z), (z, z, -v, u))
    return jnp.stack([jnp.where(special, single, pair), pair])


def second_layer(weight, bias, lanes):
    u, v = weight[0], weight[1]
    width = u.shape[0]
    z = jnp.zeros((width, lanes), u.dtype)
    wide = lambda m: jnp.pad(m, ((0, 0), (0, lanes - width)))
    u, v, m = wide(u), wide(v), wide(-v)
    rows = [(u, v, z, z), (m, u, z, z), (z, z, u, v), (z, z, m, u)]
    matrix = jnp.concatenate([jnp.concatenate(r, axis=1) for r in rows], axis=0)
    padded = jnp.pad(bias, ((0, 0), (0, lanes - width))).reshape(-1)
    return matrix, jnp.concatenate([padded, padded])[None]


def spectral_kernel(flag, x, fwd, inv, w1, b1, w2, b2, out, z, y):
    kept = fwd.shape[0] // 2
    width = w1.shape[1] // 4
    slots = x.shape[1] // (2 * width)
    lanes = w2.shape[1] // 4
    for part in range(2):
        rows = pl.ds(part * kept, kept)
        z[rows, :] = jnp.dot(fwd[rows, :], x[...], preferred_element_type=jnp.float32).astype(
            z.dtype
        )
    for s in range(slots):
        cols = pl.ds(s * 2 * width, 2 * width)
        layer = w1[min(s, 1)]
        hidden = jnp.dot(
            z[pl.ds(0, kept), cols], layer[: 2 * width], preferred_element_type=jnp.float32
        )
        hidden = hidden + jnp.dot(
            z[pl.ds(kept, kept), cols], layer[2 * width :], preferred_element_type=jnp.float32
        )
        hidden = jnp.maximum(hidden + b1[...], 0.0).astype(jnp.bfloat16)
        v = jnp.dot(hidden, w2[...], preferred_element_type=jnp.float32) + b2[...]
        v = v - jnp.minimum(jnp.maximum(v, -shrink_level), shrink_level)
        re, im, re2, im2 = [v[:, n * lanes : (n + 1) * lanes] for n in range(4)]
        top = (re + re2, im2 - im)
        bottom = (im + im2, re - re2)
        if s == 0:
            alone = flag[0] == 1
            top = (jnp.where(alone, re, top[0]), jnp.where(alone, re2, top[1]))
            bottom = (jnp.where(alone, im, bottom[0]), jnp.where(alone, im2, bottom[1]))
        for start, (a, b) in ((0, top), (kept, bottom)):
            y[pl.ds(start, kept), cols] = jnp.concatenate(
                [a[:, :width], b[:, :width]], axis=1
            ).astype(y.dtype)
    block = inv.shape[0] // 2
    for part in range(2):
        rows = pl.ds(part * block, block)
        out[rows, :] = jnp.dot(inv[rows, :], y[...], preferred_element_type=jnp.float32).astype(
            out.dtype
        )


def spectral(flag, x, fwd, inv, w1, b1, w2, b2):
    whole = pl.BlockSpec(memory_space=pltpu.VMEM)
    rows, cols = fwd.shape[0], x.shape[1]
    return pl.pallas_call(
        spectral_kernel,
        out_shape=jax.ShapeDtypeStruct(x.shape, jnp.bfloat16),
        in_specs=[pl.BlockSpec(memory_space=pltpu.SMEM)] + [whole] * 7,
        out_specs=whole,
        scratch_shapes=[pltpu.VMEM((rows, cols), jnp.bfloat16)] * 2,
        compiler_params=pltpu.CompilerParams(vmem_limit_bytes=60 * 2**20),
        name="spectral",
    )(flag, x, fwd, inv, w1, b1, w2, b2)


def per_device(grid_field, first_weight, first_bias, second_weight, second_bias):
    lon_n, lat_n = lax.axis_size("lon"), lax.axis_size("lat")
    width = first_weight.shape[2]
    local_lon, _, merged = grid_field.shape
    local_lat = merged // width
    rows = -(-local_lon // (8 * lat_n)) * 8
    lat_size = local_lat * lat_n
    everyone = lat_n * lon_n
    fwd, inv = lon_tables(lat_n, lon_n, local_lon, rows)
    lat = lat_table(lat_size)
    special = (lax.axis_index("lat") == 0) & (lax.axis_index("lon") == 0)
    w1 = first_layer(first_weight[0], special)
    b1 = jnp.concatenate([first_bias[0].reshape(-1)] * 2)[None]
    w2, b2 = second_layer(second_weight[0], second_bias[0], 128)
    flag = special.astype(jnp.int32).reshape(1)

    field = jnp.pad(grid_field[:, 0], ((0, rows * lat_n - local_lon), (0, 0)))
    field = field.reshape(lat_n, rows, merged)
    field = lax.all_to_all(field, "lat", split_axis=0, concat_axis=0, tiled=True)
    field = field.reshape(lat_n, rows, local_lat, width)
    table = jnp.asarray(lat).reshape(lat_size, lat_n, local_lat)
    comps = jnp.einsum(
        "qih,iwhc->wqc", table, field, preferred_element_type=jnp.float32
    ).astype(jnp.bfloat16)
    comps = comps.reshape(rows, everyone, -1).transpose(1, 0, 2)
    comps = lax.all_to_all(comps, group, split_axis=0, concat_axis=0, tiled=True)
    x = comps.reshape(everyone * rows, -1)
    x = spectral(flag, x, jnp.asarray(fwd), jnp.asarray(inv), w1, b1, w2, b2)
    back = x.reshape(everyone, rows, -1)
    back = lax.all_to_all(back, group, split_axis=0, concat_axis=0, tiled=True)
    back = back.transpose(1, 0, 2).reshape(rows, lat_size, width)
    mixed = jnp.einsum("qih,wqc->iwhc", table, back, preferred_element_type=jnp.float32)
    mixed = (mixed + field.astype(jnp.float32)).astype(jnp.bfloat16)
    mixed = mixed.reshape(lat_n, rows, merged)
    mixed = lax.all_to_all(mixed, "lat", split_axis=0, concat_axis=0, tiled=True)
    return mixed.reshape(lat_n * rows, merged)[:local_lon, None, :]


def solution(mesh):
    in_specs = (
        P("lon", "ch", "lat"),
        P("ch", None, None, None),
        P("ch", None, None),
        P("ch", None, None, None),
        P("ch", None, None),
    )
    return jax.shard_map(
        per_device, mesh=mesh, in_specs=in_specs, out_specs=P("lon", "ch", "lat"), check_vma=False
    )
```

```python
import functools
import math

import jax
import jax.numpy as jnp
import numpy as np
from jax import lax
from jax.experimental import pallas as pl
from jax.experimental.pallas import tpu as pltpu
from jax.sharding import PartitionSpec as P


shrink_level = 0.01
group = ("lat", "lon")


def phases(left, right, length):
    product = (left[:, None].astype(np.int64) * right[None, :]) % length
    angles = product.astype(np.float32) * np.float32(2.0 * math.pi / length)
    angles = angles.astype(np.float64)
    return np.cos(angles).astype(np.float32), np.sin(angles).astype(np.float32)


def lon_tables(lat_devices, lon_devices, local_lon, rows, chunk):
    length = local_lon * lon_devices
    kept = length // 2
    i, j, r = np.meshgrid(
        np.arange(lat_devices), np.arange(lon_devices), np.arange(*chunk), indexing="ij"
    )
    offset = (i * rows + r).reshape(-1)
    place = (j.reshape(-1) * local_lon + offset).astype(np.int64)
    real = (offset < local_lon).astype(np.float32)
    place = np.where(offset < local_lon, place, 0)
    cosine, sine = phases(np.arange(kept), place, length)
    factor = np.float32(1.0 / math.sqrt(length))
    forward = np.concatenate([cosine, -sine], axis=0) * factor * real
    weights = np.where(np.arange(kept) == 0, 1.0, 2.0).astype(np.float32)[:, None]
    inverse = np.concatenate([cosine * weights, -sine * weights], axis=0).T * factor
    inverse = inverse * real[:, None]
    return forward.astype(jnp.bfloat16), inverse.astype(jnp.bfloat16)


def lat_table(length):
    half = length // 2
    cosine, sine = phases(np.arange(half + 1), np.arange(length), length)
    sine[0] = cosine[half]
    table = np.stack([cosine[:half], sine[:half]], axis=1).reshape(length, length)
    return (table * np.float32(1.0 / math.sqrt(length))).astype(jnp.bfloat16)


def first_layer(weight, special):
    u, v = weight[0], weight[1]
    z = jnp.zeros_like(u)
    rows = lambda *blocks: jnp.concatenate([jnp.concatenate(b, axis=1) for b in blocks], axis=0)
    pair = rows((u, v, u, v), (v, -u, -v, u), (-v, u, -v, u), (u, v, -u, -v))
    single = rows((u, v, z, z), (z, z, u, v), (-v, u, z, z), (z, z, -v, u))
    return jnp.stack([jnp.where(special, single, pair), pair])


def second_layer(weight, bias, lanes):
    u, v = weight[0], weight[1]
    width = u.shape[0]
    z = jnp.zeros((width, lanes), u.dtype)
    wide = lambda m: jnp.pad(m, ((0, 0), (0, lanes - width)))
    u, v, m = wide(u), wide(v), wide(-v)
    rows = [(u, v, z, z), (m, u, z, z), (z, z, u, v), (z, z, m, u)]
    matrix = jnp.concatenate([jnp.concatenate(r, axis=1) for r in rows], axis=0)
    padded = jnp.pad(bias, ((0, 0), (0, lanes - width))).reshape(-1)
    return matrix, jnp.concatenate([padded, padded])[None]


def soft_threshold(v):
    return v - jnp.minimum(jnp.maximum(v, -shrink_level), shrink_level)


def spectral_kernel(flag, *refs, chunks):
    xs, fwds = refs[:chunks], refs[chunks : 2 * chunks]
    inv, w1, b1, w2, b2, out, y, z = refs[2 * chunks :]
    kept = fwds[0].shape[0] // 2
    width = w1.shape[1] // 4
    slots = y.shape[1] // (2 * width)
    lanes = w2.shape[1] // 4
    for part in range(2):
        rows = pl.ds(part * kept, kept)
        total = None
        for x, fwd in zip(xs, fwds):
            term = jnp.dot(fwd[rows, :], x[...], preferred_element_type=jnp.float32)
            total = term if total is None else total + term
        z[rows, :] = total.astype(z.dtype)
    for s in range(slots):
        cols = pl.ds(s * 2 * width, 2 * width)
        layer = w1[min(s, 1)]
        hidden = jnp.dot(
            z[pl.ds(0, kept), cols], layer[: 2 * width], preferred_element_type=jnp.float32
        )
        hidden = hidden + jnp.dot(
            z[pl.ds(kept, kept), cols], layer[2 * width :], preferred_element_type=jnp.float32
        )
        hidden = jnp.maximum(hidden + b1[...], 0.0).astype(jnp.bfloat16)
        v = jnp.dot(hidden, w2[...], preferred_element_type=jnp.float32) + b2[...]
        v = soft_threshold(v)
        re, im, re2, im2 = [v[:, n * lanes : (n + 1) * lanes] for n in range(4)]
        top = (re + re2, im2 - im)
        bottom = (im + im2, re - re2)
        if s == 0:
            alone = flag[0] == 1
            top = (jnp.where(alone, re, top[0]), jnp.where(alone, re2, top[1]))
            bottom = (jnp.where(alone, im, bottom[0]), jnp.where(alone, im2, bottom[1]))
        for start, (a, b) in ((0, top), (kept, bottom)):
            y[pl.ds(start, kept), cols] = jnp.concatenate(
                [a[:, :width], b[:, :width]], axis=1
            ).astype(y.dtype)
    out[...] = jnp.dot(inv[...], y[...], preferred_element_type=jnp.float32).astype(out.dtype)


def spectral(flag, xs, fwds, inv, w1, b1, w2, b2):
    whole = pl.BlockSpec(memory_space=pltpu.VMEM)
    rows, cols = fwds[0].shape[0], xs[0].shape[1]
    return pl.pallas_call(
        functools.partial(spectral_kernel, chunks=len(xs)),
        out_shape=[
            jax.ShapeDtypeStruct((inv.shape[0], cols), jnp.bfloat16),
            jax.ShapeDtypeStruct((rows, cols), jnp.bfloat16),
        ],
        in_specs=[pl.BlockSpec(memory_space=pltpu.SMEM)] + [whole] * (2 * len(xs) + 5),
        out_specs=[whole, whole],
        scratch_shapes=[pltpu.VMEM((rows, cols), jnp.bfloat16)],
        compiler_params=pltpu.CompilerParams(vmem_limit_bytes=60 * 2**20),
        cost_estimate=pl.CostEstimate(
            flops=9 * 10**9, bytes_accessed=14 * 10**6, transcendentals=0
        ),
        name="spectral",
    )(flag, *xs, *fwds, inv, w1, b1, w2, b2)


def spread(scratch, start, group, width):
    for n in range(group.shape[1] // width):
        scratch[pl.ds(start + 8 * n, 8), pl.ds(0, width)] = group[:, n * width : (n + 1) * width]


def gather(scratch, start, count, width):
    return jnp.concatenate(
        [scratch[pl.ds(start + 8 * n, 8), :][:, :width] for n in range(count)], axis=1
    )


def transform(table, source, target, size):
    for r in range(0, 8, 2):
        pair = [source[pl.ds(r + k, size, stride=8), :].astype(jnp.bfloat16) for k in range(2)]
        sums = jnp.dot(
            table[...], jnp.concatenate(pair, axis=1), preferred_element_type=jnp.float32
        )
        for k in range(2):
            target[pl.ds(r + k, size, stride=8), :] = sums[:, k * 128 : (k + 1) * 128]


def lat_forward_kernel(place, *refs, width):
    fields, (table, out, source, target) = refs[:-4], refs[-4:]
    size = table.shape[0]
    span = 4 * width
    local = size // len(fields)
    for m, field in enumerate(fields):
        base = (place[0] ^ m) * (8 * local)

        def step(g, carry, field=field, base=base):
            group = field[:, pl.ds(pl.multiple_of(g * span, 128), span)].astype(jnp.float32)
            spread(source, pl.multiple_of(base + g * 32, 8), group, width)
            return carry

        lax.fori_loop(0, local // 4, step, 0, unroll=8)
    transform(table, source, target, size)
    per = out.shape[2] // span

    def finish(d, carry):
        for p in range(per):
            start = pl.multiple_of((d * per + p) * 32, 8)
            out[d, :, pl.ds(p * span, span)] = gather(target, start, 4, width).astype(out.dtype)
        return carry

    lax.fori_loop(0, out.shape[0], finish, 0, unroll=4)


def lat_inverse_kernel(place, back, table, *refs, width, count):
    fields, outs, (source, target) = refs[:count], refs[count : 2 * count], refs[2 * count :]
    size = table.shape[0]
    span = 4 * width
    local = size // count
    per = back.shape[2] // span

    def begin(d, carry):
        for p in range(per):
            start = pl.multiple_of((d * per + p) * 32, 8)
            spread(source, start, back[d, :, pl.ds(p * span, span)].astype(jnp.float32), width)
        return carry

    lax.fori_loop(0, back.shape[0], begin, 0, unroll=4)
    transform(table, source, target, size)
    for m, (field, out) in enumerate(zip(fields, outs)):
        base = (place[0] ^ m) * (8 * local)

        def step(g, carry, field=field, out=out, base=base):
            lanes = pl.ds(pl.multiple_of(g * span, 128), span)
            sums = gather(target, pl.multiple_of(base + g * 32, 8), 4, width)
            out[:, lanes] = (sums + field[:, lanes].astype(jnp.float32)).astype(out.dtype)
            return carry

        lax.fori_loop(0, local // 4, step, 0, unroll=8)


def lat_call(kernel, args, in_specs, out_shape, out_specs, rows, size, moved):
    return pl.pallas_call(
        kernel,
        grid=(rows // 8,),
        out_shape=out_shape,
        in_specs=[pl.BlockSpec(memory_space=pltpu.SMEM)] + in_specs,
        out_specs=out_specs,
        scratch_shapes=[pltpu.VMEM((8 * size, 128), jnp.float32)] * 2,
        compiler_params=pltpu.CompilerParams(vmem_limit_bytes=40 * 2**20),
        cost_estimate=pl.CostEstimate(
            flops=2 * rows * size * size * 128, bytes_accessed=2 * moved, transcendentals=0
        ),
    )(*args)


def lat_forward(place, fields, table, everyone, width):
    rows, merged = fields[0].shape
    size = table.shape[0]
    lanes = size * width // everyone
    strip = pl.BlockSpec((8, merged), lambda n: (n, 0))
    return lat_call(
        functools.partial(lat_forward_kernel, width=width),
        (place, *fields, table),
        [strip] * len(fields) + [pl.BlockSpec((size, size), lambda n: (0, 0))],
        jax.ShapeDtypeStruct((everyone, rows, lanes), jnp.bfloat16),
        pl.BlockSpec((everyone, 8, lanes), lambda n: (0, n, 0)),
        rows,
        size,
        rows * size * width * 2,
    )


def lat_inverse(place, back, table, fields, width):
    everyone, rows, lanes = back.shape
    size = table.shape[0]
    merged = fields[0].shape[1]
    strip = pl.BlockSpec((8, merged), lambda n: (n, 0))
    return lat_call(
        functools.partial(lat_inverse_kernel, width=width, count=len(fields)),
        (place, back, table, *fields),
        [
            pl.BlockSpec((everyone, 8, lanes), lambda n: (0, n, 0)),
            pl.BlockSpec((size, size), lambda n: (0, 0)),
        ]
        + [strip] * len(fields),
        [jax.ShapeDtypeStruct((rows, merged), jnp.bfloat16)] * len(fields),
        [strip] * len(fields),
        rows,
        size,
        rows * size * width * 2,
    )


def assemble_kernel(place, *refs, chunks, count):
    pieces, out = refs[:-1], refs[-1]
    rows, length = chunks[-1][1], out.shape[0]
    for n, (start, stop) in enumerate(chunks):
        for m in range(count):
            piece = pieces[n * count + m]
            block = place[0] ^ m
            rest = length - (count - 1) * rows - start

            def fill(piece=piece, block=block, start=start, stop=stop):
                row = pl.multiple_of(block * rows + start, 8)
                out[pl.ds(row, stop - start), :] = piece[...]

            if rest >= stop - start:
                fill()
            else:
                pl.when(block < count - 1)(fill)

                @pl.when(block == count - 1)
                def _(piece=piece, rest=rest):
                    out[pl.ds(length - rest, rest), :] = piece[pl.ds(0, rest), :]


def assemble(place, mixed, chunks, length):
    whole = pl.BlockSpec(memory_space=pltpu.VMEM)
    pieces = [piece for chunk in mixed for piece in chunk]
    return pl.pallas_call(
        functools.partial(assemble_kernel, chunks=chunks, count=len(mixed[0])),
        out_shape=jax.ShapeDtypeStruct((length, pieces[0].shape[1]), jnp.bfloat16),
        in_specs=[pl.BlockSpec(memory_space=pltpu.SMEM)] + [whole] * len(pieces),
        out_specs=whole,
        compiler_params=pltpu.CompilerParams(vmem_limit_bytes=16 * 2**20),
        cost_estimate=pl.CostEstimate(flops=0, bytes_accessed=5 * 10**6, transcendentals=0),
        name="assemble",
    )(place, *pieces)


def swap(pieces, count):
    return [pieces[0]] + [
        lax.ppermute(pieces[m], "lat", [(i, i ^ m) for i in range(count)]) for m in range(1, count)
    ]


def layer(grid_field, first_weight, first_bias, second_weight, second_bias):
    lon_n, lat_n = lax.axis_size("lon"), lax.axis_size("lat")
    width = first_weight.shape[2]
    local_lon, _, merged = grid_field.shape
    local_lat = merged // width
    rows = -(-local_lon // (8 * lat_n)) * 8
    lat_size = local_lat * lat_n
    everyone = lat_n * lon_n
    chunks = ((0, 8), (8, rows))
    tables = [lon_tables(lat_n, lon_n, local_lon, rows, c) for c in chunks]
    fwds = [jnp.asarray(t[0]) for t in tables]
    invs = [jnp.asarray(t[1]) for t in tables]
    lat = lat_table(lat_size)
    lat, lat_back = jnp.asarray(lat), jnp.asarray(np.ascontiguousarray(lat.T))
    special = (lax.axis_index("lat") == 0) & (lax.axis_index("lon") == 0)
    w1 = first_layer(first_weight[0], special)
    b1 = jnp.concatenate([first_bias[0].reshape(-1)] * 2)[None]
    w2, b2 = second_layer(second_weight[0], second_bias[0], 128)
    flag = special.astype(jnp.int32).reshape(1)
    me = lax.axis_index("lat")
    place = me.astype(jnp.int32).reshape(1)

    field = grid_field[:, 0]
    padded = jnp.pad(field, ((0, rows * lat_n - local_lon), (0, 0)))
    exchange = lambda x: lax.all_to_all(x, group, split_axis=0, concat_axis=0, tiled=True)
    flat = lambda x: x.reshape(-1, x.shape[-1])

    fields, xs = [], []
    for start, stop in chunks:
        whole = padded if (lat_n - 1) * rows + stop > local_lon else field
        pieces = [
            lax.dynamic_slice(whole, (rows * (me ^ m) + start, 0), (stop - start, merged))
            for m in range(lat_n)
        ]
        fields.append(swap(pieces, lat_n))
        xs.append(lat_forward(place, fields[-1], lat, everyone, width))
    for n in range(2):
        xs[n] = exchange(xs[n])
    last, y = spectral(flag, [flat(x) for x in xs], fwds, invs[1], w1, b1, w2, b2)
    outs = [None, last]
    outs[0] = jnp.dot(invs[0], y, preferred_element_type=jnp.float32).astype(jnp.bfloat16)
    mixed, backs = [None, None], [None, None]
    for n in (1, 0):
        if n == 0:
            outs[0], backs[1] = lax.optimization_barrier((outs[0], backs[1]))
        backs[n] = exchange(outs[n].reshape(everyone, chunks[n][1] - chunks[n][0], -1))
    for n in (1, 0):
        start, stop = chunks[n]
        pieces = lat_inverse(place, backs[n], lat_back, fields[n], width)
        mixed[n] = swap(pieces, lat_n)
    return assemble(place, mixed, chunks, local_lon)[:, None, :]


def solution(mesh):
    in_specs = (
        P("lon", "ch", "lat"),
        P("ch", None, None, None),
        P("ch", None, None),
        P("ch", None, None, None),
        P("ch", None, None),
    )
    return jax.shard_map(
        layer, mesh=mesh, in_specs=in_specs, out_specs=P("lon", "ch", "lat"), check_vma=False
    )
```

```python
import functools
import math

import jax
import jax.numpy as jnp
import numpy as np
from jax import lax
from jax.experimental import pallas as pl
from jax.experimental.pallas import tpu as pltpu
from jax.sharding import PartitionSpec as P


shrink_level = 0.01
group = ("lat", "lon")
LIMITS = (40, 62)


def phases(left, right, length):
    product = (left[:, None].astype(np.int64) * right[None, :]) % length
    angles = product.astype(np.float32) * np.float32(2.0 * math.pi / length)
    angles = angles.astype(np.float64)
    return np.cos(angles).astype(np.float32), np.sin(angles).astype(np.float32)


def lon_tables(lat_devices, lon_devices, local_lon, rows, chunk):
    length = local_lon * lon_devices
    kept = length // 2
    i, j, r = np.meshgrid(
        np.arange(lat_devices), np.arange(lon_devices), np.arange(*chunk), indexing="ij"
    )
    offset = (i * rows + r).reshape(-1)
    place = (j.reshape(-1) * local_lon + offset).astype(np.int64)
    real = (offset < local_lon).astype(np.float32)
    place = np.where(offset < local_lon, place, 0)
    cosine, sine = phases(np.arange(kept), place, length)
    factor = np.float32(1.0 / math.sqrt(length))
    forward = np.concatenate([cosine, -sine], axis=0) * factor * real
    weights = np.where(np.arange(kept) == 0, 1.0, 2.0).astype(np.float32)[:, None]
    inverse = np.concatenate([cosine * weights, -sine * weights], axis=0).T * factor
    inverse = inverse * real[:, None]
    return forward.astype(jnp.bfloat16), inverse.astype(jnp.bfloat16)


def lat_table(length):
    half = length // 2
    cosine, sine = phases(np.arange(half + 1), np.arange(length), length)
    sine[0] = cosine[half]
    table = np.stack([cosine[:half], sine[:half]], axis=1).reshape(length, length)
    return (table * np.float32(1.0 / math.sqrt(length))).astype(jnp.bfloat16)


def first_layer(weight, special):
    u, v = weight[0], weight[1]
    z = jnp.zeros_like(u)
    rows = lambda *blocks: jnp.concatenate([jnp.concatenate(b, axis=1) for b in blocks], axis=0)
    pair = rows((u, v, u, v), (v, -u, -v, u), (-v, u, -v, u), (u, v, -u, -v))
    single = rows((u, v, z, z), (z, z, u, v), (-v, u, z, z), (z, z, -v, u))
    return jnp.stack([jnp.where(special, single, pair), pair])


def second_layer(weight, bias, lanes):
    u, v = weight[0], weight[1]
    width = u.shape[0]
    z = jnp.zeros((width, lanes), u.dtype)
    wide = lambda m: jnp.pad(m, ((0, 0), (0, lanes - width)))
    u, v, m = wide(u), wide(v), wide(-v)
    rows = [(u, v, z, z), (m, u, z, z), (z, z, u, v), (z, z, m, u)]
    matrix = jnp.concatenate([jnp.concatenate(r, axis=1) for r in rows], axis=0)
    padded = jnp.pad(bias, ((0, 0), (0, lanes - width))).reshape(-1)
    return matrix, jnp.concatenate([padded, padded])[None]


def soft_threshold(v):
    return v - jnp.minimum(jnp.maximum(v, -shrink_level), shrink_level)


def spectral_kernel(flag, *refs, chunks):
    xs, fwds = refs[:chunks], refs[chunks : 2 * chunks]
    inv, w1, b1, w2, b2, out, y, z = refs[2 * chunks :]
    kept = fwds[0].shape[0] // 2
    width = w1.shape[1] // 4
    slots = y.shape[1] // (2 * width)
    lanes = w2.shape[1] // 4
    for part in range(2):
        rows = pl.ds(part * kept, kept)
        total = None
        for x, fwd in zip(xs, fwds):
            term = jnp.dot(fwd[rows, :], x[...], preferred_element_type=jnp.float32)
            total = term if total is None else total + term
        z[rows, :] = total.astype(z.dtype)
    for s in range(slots):
        cols = pl.ds(s * 2 * width, 2 * width)
        layer = w1[min(s, 1)]
        hidden = jnp.dot(
            z[pl.ds(0, kept), cols], layer[: 2 * width], preferred_element_type=jnp.float32
        )
        hidden = hidden + jnp.dot(
            z[pl.ds(kept, kept), cols], layer[2 * width :], preferred_element_type=jnp.float32
        )
        hidden = jnp.maximum(hidden + b1[...], 0.0).astype(jnp.bfloat16)
        v = jnp.dot(hidden, w2[...], preferred_element_type=jnp.float32) + b2[...]
        v = soft_threshold(v)
        re, im, re2, im2 = [v[:, n * lanes : (n + 1) * lanes] for n in range(4)]
        top = (re + re2, im2 - im)
        bottom = (im + im2, re - re2)
        if s == 0:
            alone = flag[0] == 1
            top = (jnp.where(alone, re, top[0]), jnp.where(alone, re2, top[1]))
            bottom = (jnp.where(alone, im, bottom[0]), jnp.where(alone, im2, bottom[1]))
        for start, (a, b) in ((0, top), (kept, bottom)):
            y[pl.ds(start, kept), cols] = jnp.concatenate(
                [a[:, :width], b[:, :width]], axis=1
            ).astype(y.dtype)
    out[...] = jnp.dot(inv[...], y[...], preferred_element_type=jnp.float32).astype(out.dtype)


def unwind_kernel(inv, y, out):
    out[...] = jnp.dot(inv[...], y[...], preferred_element_type=jnp.float32).astype(out.dtype)


def unwind(inv, y):
    whole = pl.BlockSpec(memory_space=pltpu.VMEM)
    return pl.pallas_call(
        unwind_kernel,
        out_shape=jax.ShapeDtypeStruct((inv.shape[0], y.shape[1]), jnp.bfloat16),
        in_specs=[whole] * 2,
        out_specs=whole,
        compiler_params=pltpu.CompilerParams(vmem_limit_bytes=62 * 2**20),
        cost_estimate=pl.CostEstimate(
            flops=10**9, bytes_accessed=4 * 10**6, transcendentals=0
        ),
        name="unwind",
    )(inv, y)


def spectral(flag, xs, fwds, inv, w1, b1, w2, b2):
    whole = pl.BlockSpec(memory_space=pltpu.VMEM)
    rows, cols = fwds[0].shape[0], xs[0].shape[1]
    return pl.pallas_call(
        functools.partial(spectral_kernel, chunks=len(xs)),
        out_shape=[
            jax.ShapeDtypeStruct((inv.shape[0], cols), jnp.bfloat16),
            jax.ShapeDtypeStruct((rows, cols), jnp.bfloat16),
        ],
        in_specs=[pl.BlockSpec(memory_space=pltpu.SMEM)] + [whole] * (2 * len(xs) + 5),
        out_specs=[whole, whole],
        scratch_shapes=[pltpu.VMEM((rows, cols), jnp.bfloat16)],
        compiler_params=pltpu.CompilerParams(vmem_limit_bytes=60 * 2**20),
        cost_estimate=pl.CostEstimate(
            flops=9 * 10**9, bytes_accessed=14 * 10**6, transcendentals=0
        ),
        name="spectral",
    )(flag, *xs, *fwds, inv, w1, b1, w2, b2)


def spread(scratch, start, group, width):
    for n in range(group.shape[1] // width):
        scratch[pl.ds(start + 8 * n, 8), pl.ds(0, width)] = group[:, n * width : (n + 1) * width]


def gather(scratch, start, count, width):
    return jnp.concatenate(
        [scratch[pl.ds(start + 8 * n, 8), :][:, :width] for n in range(count)], axis=1
    )


def transform(table, source, target, size):
    for r in range(0, 8, 2):
        pair = [source[pl.ds(r + k, size, stride=8), :].astype(jnp.bfloat16) for k in range(2)]
        sums = jnp.dot(
            table[...], jnp.concatenate(pair, axis=1), preferred_element_type=jnp.float32
        )
        for k in range(2):
            target[pl.ds(r + k, size, stride=8), :] = sums[:, k * 128 : (k + 1) * 128]


def lat_forward_kernel(place, *refs, width):
    fields, (table, out, source, target) = refs[:-4], refs[-4:]
    size = table.shape[0]
    span = 4 * width
    local = size // len(fields)
    bases = [(place[0] ^ m) * (8 * local) for m in range(len(fields))]

    def step(g, carry):
        lanes = pl.ds(pl.multiple_of(g * span, 128), span)
        for field, base in zip(fields, bases):
            start = pl.multiple_of(base + g * 32, 8)
            spread(source, start, field[:, lanes].astype(jnp.float32), width)
        return carry

    lax.fori_loop(0, local // 4, step, 0, unroll=8)
    transform(table, source, target, size)
    per = out.shape[2] // span

    def finish(d, carry):
        for p in range(per):
            start = pl.multiple_of((d * per + p) * 32, 8)
            out[d, :, pl.ds(p * span, span)] = gather(target, start, 4, width).astype(out.dtype)
        return carry

    lax.fori_loop(0, out.shape[0], finish, 0, unroll=16)


def lat_inverse_kernel(place, back, table, *refs, width, count):
    fields, outs, (source, target) = refs[:count], refs[count : 2 * count], refs[2 * count :]
    size = table.shape[0]
    span = 4 * width
    local = size // count
    per = back.shape[2] // span

    def begin(d, carry):
        for p in range(per):
            start = pl.multiple_of((d * per + p) * 32, 8)
            spread(source, start, back[d, :, pl.ds(p * span, span)].astype(jnp.float32), width)
        return carry

    lax.fori_loop(0, back.shape[0], begin, 0, unroll=16)
    transform(table, source, target, size)
    bases = [(place[0] ^ m) * (8 * local) for m in range(count)]

    def step(g, carry):
        lanes = pl.ds(pl.multiple_of(g * span, 128), span)
        for field, out, base in zip(fields, outs, bases):
            sums = gather(target, pl.multiple_of(base + g * 32, 8), 4, width)
            out[:, lanes] = (sums + field[:, lanes].astype(jnp.float32)).astype(out.dtype)
        return carry

    lax.fori_loop(0, local // 4, step, 0, unroll=8)


def lat_call(kernel, args, in_specs, out_shape, out_specs, rows, size, moved, limit=40):
    return pl.pallas_call(
        kernel,
        grid=(rows // 8,),
        out_shape=out_shape,
        in_specs=[pl.BlockSpec(memory_space=pltpu.SMEM)] + in_specs,
        out_specs=out_specs,
        scratch_shapes=[pltpu.VMEM((8 * size, 128), jnp.float32)] * 2,
        compiler_params=pltpu.CompilerParams(vmem_limit_bytes=limit * 2**20),
        cost_estimate=pl.CostEstimate(
            flops=2 * rows * size * size * 128, bytes_accessed=2 * moved, transcendentals=0
        ),
    )(*args)


def lat_forward(place, fields, table, everyone, width):
    rows, merged = fields[0].shape
    size = table.shape[0]
    lanes = size * width // everyone
    strip = pl.BlockSpec((8, merged), lambda n: (n, 0))
    return lat_call(
        functools.partial(lat_forward_kernel, width=width),
        (place, *fields, table),
        [strip] * len(fields) + [pl.BlockSpec((size, size), lambda n: (0, 0))],
        jax.ShapeDtypeStruct((everyone, rows, lanes), jnp.bfloat16),
        pl.BlockSpec((everyone, 8, lanes), lambda n: (0, n, 0)),
        rows,
        size,
        rows * size * width * 2,
    )


def lat_inverse(place, back, table, fields, width, tile, limit):
    everyone, _, lanes = back.shape
    size = table.shape[0]
    merged = fields[0].shape[1]
    strip = pl.BlockSpec((8, merged), lambda n: (n, 0))
    return lat_call(
        functools.partial(lat_inverse_kernel, width=width, count=len(fields)),
        (place, back, table, *fields),
        [
            pl.BlockSpec((everyone, 8, lanes), lambda n: (0, n + tile, 0)),
            pl.BlockSpec((size, size), lambda n: (0, 0)),
        ]
        + [pl.BlockSpec((8, merged), lambda n: (n + tile, 0))] * len(fields),
        [jax.ShapeDtypeStruct((8, merged), jnp.bfloat16)] * len(fields),
        [strip] * len(fields),
        8,
        size,
        8 * size * width * 2,
        limit,
    )


def assemble_kernel(place, *refs, chunks, rows, count):
    pieces, out = refs[:-1], refs[-1]
    length = out.shape[0]
    for n, (start, stop) in enumerate(chunks):
        for m in range(count):
            piece = pieces[n * count + m]
            block = place[0] ^ m
            rest = length - (count - 1) * rows - start

            def fill(piece=piece, block=block, start=start, stop=stop):
                row = pl.multiple_of(block * rows + start, 8)
                out[pl.ds(row, stop - start), :] = piece[...]

            if rest >= stop - start:
                fill()
            else:
                pl.when(block < count - 1)(fill)

                @pl.when(block == count - 1)
                def _(piece=piece, rest=rest):
                    out[pl.ds(length - rest, rest), :] = piece[pl.ds(0, rest), :]


def insert_kernel(place, *refs, start, rows, count):
    pieces, out, sems = refs[:count], refs[-2], refs[-1]
    copies = []
    for m in range(count):
        row = pl.multiple_of((place[0] ^ m) * rows + start, 8)
        copies.append(
            pltpu.make_async_copy(pieces[m], out.at[pl.ds(row, pieces[m].shape[0])], sems.at[m])
        )
        copies[-1].start()
    for copy in copies:
        copy.wait()


def assemble(place, mixed, chunks, rows, length):
    whole, away = pl.BlockSpec(memory_space=pltpu.VMEM), pl.BlockSpec(memory_space=pl.ANY)
    scalar = pl.BlockSpec(memory_space=pltpu.SMEM)
    pieces = [piece for chunk in mixed[:-1] for piece in chunk]
    count = len(mixed[0])
    shape = jax.ShapeDtypeStruct((length, pieces[0].shape[1]), jnp.bfloat16)
    most = pl.pallas_call(
        functools.partial(assemble_kernel, chunks=chunks[:-1], rows=rows, count=count),
        out_shape=shape,
        in_specs=[scalar] + [whole] * len(pieces),
        out_specs=whole,
        compiler_params=pltpu.CompilerParams(vmem_limit_bytes=16 * 2**20),
        cost_estimate=pl.CostEstimate(flops=0, bytes_accessed=5 * 10**6, transcendentals=0),
        name="assemble",
    )(place, *pieces)
    return pl.pallas_call(
        functools.partial(insert_kernel, start=chunks[-1][0], rows=rows, count=count),
        out_shape=shape,
        in_specs=[scalar] + [whole] * count + [away],
        out_specs=away,
        input_output_aliases={1 + count: 0},
        scratch_shapes=[pltpu.SemaphoreType.DMA((count,))],
        compiler_params=pltpu.CompilerParams(vmem_limit_bytes=16 * 2**20),
        cost_estimate=pl.CostEstimate(flops=0, bytes_accessed=2 * 10**6, transcendentals=0),
        name="insert",
    )(place, *mixed[-1], most)


def swap(pieces, count):
    return [pieces[0]] + [
        lax.ppermute(pieces[m], "lat", [(i, i ^ m) for i in range(count)]) for m in range(1, count)
    ]


def layer(grid_field, first_weight, first_bias, second_weight, second_bias):
    lon_n, lat_n = lax.axis_size("lon"), lax.axis_size("lat")
    width = first_weight.shape[2]
    local_lon, _, merged = grid_field.shape
    local_lat = merged // width
    rows = -(-local_lon // (8 * lat_n)) * 8
    lat_size = local_lat * lat_n
    everyone = lat_n * lon_n
    chunks = ((0, 8), (8, rows))
    tables = [lon_tables(lat_n, lon_n, local_lon, rows, c) for c in chunks]
    fwds = [jnp.asarray(t[0]) for t in tables]
    invs = [jnp.asarray(t[1]) for t in tables]
    lat = lat_table(lat_size)
    lat, lat_back = jnp.asarray(lat), jnp.asarray(np.ascontiguousarray(lat.T))
    special = (lax.axis_index("lat") == 0) & (lax.axis_index("lon") == 0)
    w1 = first_layer(first_weight[0], special)
    b1 = jnp.concatenate([first_bias[0].reshape(-1)] * 2)[None]
    w2, b2 = second_layer(second_weight[0], second_bias[0], 128)
    flag = special.astype(jnp.int32).reshape(1)
    me = lax.axis_index("lat")
    place = me.astype(jnp.int32).reshape(1)

    field = grid_field[:, 0]
    padded = jnp.pad(field, ((0, rows * lat_n - local_lon), (0, 0)))
    exchange = lambda x: lax.all_to_all(x, group, split_axis=0, concat_axis=0, tiled=True)
    flat = lambda x: x.reshape(-1, x.shape[-1])

    fields, xs = [], []
    for start, stop in chunks:
        whole = padded if (lat_n - 1) * rows + stop > local_lon else field
        pieces = [
            lax.dynamic_slice(whole, (rows * (me ^ m) + start, 0), (stop - start, merged))
            for m in range(lat_n)
        ]
        fields.append(swap(pieces, lat_n))
        xs.append(lat_forward(place, fields[-1], lat, everyone, width))
    for n in range(2):
        xs[n] = exchange(xs[n])
    last, y = spectral(flag, [flat(x) for x in xs], fwds, invs[1], w1, b1, w2, b2)
    outs = [None, last]
    outs[0] = unwind(invs[0], y)
    backs = [None, None]
    for n in (1, 0):
        if n == 0:
            outs[0], backs[1] = lax.optimization_barrier((outs[0], backs[1]))
        backs[n] = exchange(outs[n].reshape(everyone, chunks[n][1] - chunks[n][0], -1))
    strips, mixed = [], []
    for n in (1, 0):
        start, stop = chunks[n]
        for first in range(start, stop, 8):
            pieces = lat_inverse(
                place, backs[n], lat_back, fields[n], width, (first - start) // 8, LIMITS[n]
            )
            mixed.append(swap(pieces, lat_n))
            strips.append((first, first + 8))
    return assemble(place, mixed, strips, rows, local_lon)[:, None, :]


def solution(mesh):
    in_specs = (
        P("lon", "ch", "lat"),
        P("ch", None, None, None),
        P("ch", None, None),
        P("ch", None, None, None),
        P("ch", None, None),
    )
    return jax.shard_map(
        layer, mesh=mesh, in_specs=in_specs, out_specs=P("lon", "ch", "lat"), check_vma=False
    )
```

```python
import functools
import math

import jax
import jax.numpy as jnp
import numpy as np
from jax import lax
from jax.experimental import pallas as pl
from jax.experimental.pallas import tpu as pltpu
from jax.sharding import PartitionSpec as P


shrink_level = 0.01
group = ("lat", "lon")
LIMITS = (40, 62)


def phases(left, right, length):
    product = (left[:, None].astype(np.int64) * right[None, :]) % length
    angles = product.astype(np.float32) * np.float32(2.0 * math.pi / length)
    angles = angles.astype(np.float64)
    return np.cos(angles).astype(np.float32), np.sin(angles).astype(np.float32)


def lon_tables(lat_devices, lon_devices, local_lon, rows, chunk):
    length = local_lon * lon_devices
    i, j, r = np.meshgrid(
        np.arange(lat_devices), np.arange(lon_devices // 2), np.arange(*chunk), indexing="ij"
    )
    offset = (i * rows + r).reshape(-1)
    place = (j.reshape(-1) * local_lon + offset).astype(np.int64)
    real = (offset < local_lon).astype(np.float32)
    place = np.where(offset < local_lon, place, 0)
    factor = np.float32(1.0 / math.sqrt(length))
    forward, inverse = [], []
    for parity in range(2):
        modes = np.arange(parity, length // 2, 2)
        cosine, sine = phases(modes, place, length)
        extra = ((0, -len(modes) % 16), (0, 0))
        stack = lambda c, q: np.concatenate([np.pad(c, extra), np.pad(-q, extra)], axis=0)
        weights = np.where(modes == 0, 1.0, 2.0).astype(np.float32)[:, None]
        forward.append(stack(cosine, sine) * factor * real)
        inverse.append((stack(cosine * weights, sine * weights) * factor * real).T)
    return np.stack(forward).astype(jnp.bfloat16), np.stack(inverse).astype(jnp.bfloat16)


def lat_table(length):
    half = length // 2
    cosine, sine = phases(np.arange(half + 1), np.arange(length), length)
    sine[0] = cosine[half]
    table = np.stack([cosine[:half], sine[:half]], axis=1).reshape(length, length)
    return (table * np.float32(1.0 / math.sqrt(length))).astype(jnp.bfloat16)


def first_layer(weight, special):
    u, v = weight[0], weight[1]
    z = jnp.zeros_like(u)
    rows = lambda *blocks: jnp.concatenate([jnp.concatenate(b, axis=1) for b in blocks], axis=0)
    pair = rows((u, v, u, v), (v, -u, -v, u), (-v, u, -v, u), (u, v, -u, -v))
    single = rows((u, v, z, z), (z, z, u, v), (-v, u, z, z), (z, z, -v, u))
    return jnp.stack([jnp.where(special, single, pair), pair])


def second_layer(weight, bias, lanes):
    u, v = weight[0], weight[1]
    width = u.shape[0]
    z = jnp.zeros((width, lanes), u.dtype)
    wide = lambda m: jnp.pad(m, ((0, 0), (0, lanes - width)))
    u, v, m = wide(u), wide(v), wide(-v)
    rows = [(u, v, z, z), (m, u, z, z), (z, z, u, v), (z, z, m, u)]
    matrix = jnp.concatenate([jnp.concatenate(r, axis=1) for r in rows], axis=0)
    padded = jnp.pad(bias, ((0, 0), (0, lanes - width))).reshape(-1)
    return matrix, jnp.concatenate([padded, padded])[None]


def soft_threshold(v):
    return v - jnp.minimum(jnp.maximum(v, -shrink_level), shrink_level)


def fold(x, blocks):
    half = x.shape[0] // (2 * blocks)
    near, far = [
        jnp.concatenate(
            [x[pl.ds((2 * n + side) * half, half), :].astype(jnp.float32) for n in range(blocks)],
            axis=0,
        )
        for side in range(2)
    ]
    return (near + far).astype(jnp.bfloat16), (near - far).astype(jnp.bfloat16)


def unfold(inv, y, out, blocks):
    count = inv.shape[2]
    even, odd = [
        jnp.dot(inv[p], y[pl.ds(p * count, count), :], preferred_element_type=jnp.float32)
        for p in range(2)
    ]
    near, far = (even + odd).astype(out.dtype), (even - odd).astype(out.dtype)
    half = out.shape[0] // (2 * blocks)
    for n in range(blocks):
        out[pl.ds(2 * n * half, half), :] = near[n * half : (n + 1) * half]
        out[pl.ds((2 * n + 1) * half, half), :] = far[n * half : (n + 1) * half]


def spectral_kernel(flag, *refs, chunks, blocks):
    xs, fwds = refs[:chunks], refs[chunks : 2 * chunks]
    inv, w1, b1, w2, b2, out, y, z = refs[2 * chunks :]
    count = fwds[0].shape[1]
    kept = count // 2
    width = w1.shape[1] // 4
    slots = y.shape[1] // (2 * width)
    lanes = w2.shape[1] // 4
    folded = [fold(x, blocks) for x in xs]
    for p in range(2):
        total = None
        for fwd, pair in zip(fwds, folded):
            term = jnp.dot(fwd[p], pair[p], preferred_element_type=jnp.float32)
            total = term if total is None else total + term
        z[pl.ds(p * count, count), :] = total.astype(z.dtype)
    for base, s in [(p * count, s) for p in range(2) for s in range(slots)]:
        cols = pl.ds(s * 2 * width, 2 * width)
        layer = w1[min(s, 1)]
        hidden = jnp.dot(
            z[pl.ds(base, kept), cols], layer[: 2 * width], preferred_element_type=jnp.float32
        )
        hidden = hidden + jnp.dot(
            z[pl.ds(base + kept, kept), cols], layer[2 * width :], preferred_element_type=jnp.float32
        )
        hidden = jnp.maximum(hidden + b1[...], 0.0).astype(jnp.bfloat16)
        v = jnp.dot(hidden, w2[...], preferred_element_type=jnp.float32) + b2[...]
        v = soft_threshold(v)
        re, im, re2, im2 = [v[:, n * lanes : (n + 1) * lanes] for n in range(4)]
        top = (re + re2, im2 - im)
        bottom = (im + im2, re - re2)
        if s == 0:
            alone = flag[0] == 1
            top = (jnp.where(alone, re, top[0]), jnp.where(alone, re2, top[1]))
            bottom = (jnp.where(alone, im, bottom[0]), jnp.where(alone, im2, bottom[1]))
        for start, (a, b) in ((base, top), (base + kept, bottom)):
            y[pl.ds(start, kept), cols] = jnp.concatenate(
                [a[:, :width], b[:, :width]], axis=1
            ).astype(y.dtype)
    unfold(inv, y, out, blocks)


def unwind_kernel(inv, y, out, *, blocks):
    unfold(inv, y, out, blocks)


def unwind(inv, y, blocks):
    whole = pl.BlockSpec(memory_space=pltpu.VMEM)
    return pl.pallas_call(
        functools.partial(unwind_kernel, blocks=blocks),
        out_shape=jax.ShapeDtypeStruct((2 * inv.shape[1], y.shape[1]), jnp.bfloat16),
        in_specs=[whole] * 2,
        out_specs=whole,
        compiler_params=pltpu.CompilerParams(vmem_limit_bytes=62 * 2**20),
        cost_estimate=pl.CostEstimate(
            flops=10**9, bytes_accessed=4 * 10**6, transcendentals=0
        ),
        name="unwind",
    )(inv, y)


def spectral(flag, xs, fwds, inv, w1, b1, w2, b2, blocks):
    whole = pl.BlockSpec(memory_space=pltpu.VMEM)
    rows, cols = 2 * fwds[0].shape[1], xs[0].shape[1]
    return pl.pallas_call(
        functools.partial(spectral_kernel, chunks=len(xs), blocks=blocks),
        out_shape=[
            jax.ShapeDtypeStruct((2 * inv.shape[1], cols), jnp.bfloat16),
            jax.ShapeDtypeStruct((rows, cols), jnp.bfloat16),
        ],
        in_specs=[pl.BlockSpec(memory_space=pltpu.SMEM)] + [whole] * (2 * len(xs) + 5),
        out_specs=[whole, whole],
        scratch_shapes=[pltpu.VMEM((rows, cols), jnp.bfloat16)],
        compiler_params=pltpu.CompilerParams(vmem_limit_bytes=60 * 2**20),
        cost_estimate=pl.CostEstimate(
            flops=9 * 10**9, bytes_accessed=14 * 10**6, transcendentals=0
        ),
        name="spectral",
    )(flag, *xs, *fwds, inv, w1, b1, w2, b2)


def spread(scratch, start, group, width):
    for n in range(group.shape[1] // width):
        scratch[pl.ds(start + 8 * n, 8), pl.ds(0, width)] = group[:, n * width : (n + 1) * width]


def gather(scratch, start, count, width):
    return jnp.concatenate(
        [scratch[pl.ds(start + 8 * n, 8), :][:, :width] for n in range(count)], axis=1
    )


def transform(table, source, target, size):
    for r in range(0, 8, 2):
        pair = [source[pl.ds(r + k, size, stride=8), :].astype(jnp.bfloat16) for k in range(2)]
        sums = jnp.dot(
            table[...], jnp.concatenate(pair, axis=1), preferred_element_type=jnp.float32
        )
        for k in range(2):
            target[pl.ds(r + k, size, stride=8), :] = sums[:, k * 128 : (k + 1) * 128]


def lat_forward_kernel(place, *refs, width):
    fields, (table, out, source, target) = refs[:-4], refs[-4:]
    size = table.shape[0]
    span = 4 * width
    local = size // len(fields)
    bases = [(place[0] ^ m) * (8 * local) for m in range(len(fields))]

    def step(g, carry):
        lanes = pl.ds(pl.multiple_of(g * span, 128), span)
        for field, base in zip(fields, bases):
            start = pl.multiple_of(base + g * 32, 8)
            spread(source, start, field[:, lanes].astype(jnp.float32), width)
        return carry

    lax.fori_loop(0, local // 4, step, 0, unroll=8)
    transform(table, source, target, size)
    per = out.shape[2] // span

    def finish(d, carry):
        for p in range(per):
            start = pl.multiple_of((d * per + p) * 32, 8)
            out[d, :, pl.ds(p * span, span)] = gather(target, start, 4, width).astype(out.dtype)
        return carry

    lax.fori_loop(0, out.shape[0], finish, 0, unroll=16)


def lat_inverse_kernel(place, back, table, *refs, width, count):
    fields, outs, (source, target) = refs[:count], refs[count : 2 * count], refs[2 * count :]
    size = table.shape[0]
    span = 4 * width
    local = size // count
    per = back.shape[2] // span

    def begin(d, carry):
        for p in range(per):
            start = pl.multiple_of((d * per + p) * 32, 8)
            spread(source, start, back[d, :, pl.ds(p * span, span)].astype(jnp.float32), width)
        return carry

    lax.fori_loop(0, back.shape[0], begin, 0, unroll=16)
    transform(table, source, target, size)
    bases = [(place[0] ^ m) * (8 * local) for m in range(count)]

    def step(g, carry):
        lanes = pl.ds(pl.multiple_of(g * span, 128), span)
        for field, out, base in zip(fields, outs, bases):
            sums = gather(target, pl.multiple_of(base + g * 32, 8), 4, width)
            out[:, lanes] = (sums + field[:, lanes].astype(jnp.float32)).astype(out.dtype)
        return carry

    lax.fori_loop(0, local // 4, step, 0, unroll=8)


def lat_call(kernel, args, in_specs, out_shape, out_specs, rows, size, moved, limit=40):
    return pl.pallas_call(
        kernel,
        grid=(rows // 8,),
        out_shape=out_shape,
        in_specs=[pl.BlockSpec(memory_space=pltpu.SMEM)] + in_specs,
        out_specs=out_specs,
        scratch_shapes=[pltpu.VMEM((8 * size, 128), jnp.float32)] * 2,
        compiler_params=pltpu.CompilerParams(vmem_limit_bytes=limit * 2**20),
        cost_estimate=pl.CostEstimate(
            flops=2 * rows * size * size * 128, bytes_accessed=2 * moved, transcendentals=0
        ),
    )(*args)


def lat_forward(place, fields, table, everyone, width):
    rows, merged = fields[0].shape
    size = table.shape[0]
    lanes = size * width // everyone
    strip = pl.BlockSpec((8, merged), lambda n: (n, 0))
    return lat_call(
        functools.partial(lat_forward_kernel, width=width),
        (place, *fields, table),
        [strip] * len(fields) + [pl.BlockSpec((size, size), lambda n: (0, 0))],
        jax.ShapeDtypeStruct((everyone, rows, lanes), jnp.bfloat16),
        pl.BlockSpec((everyone, 8, lanes), lambda n: (0, n, 0)),
        rows,
        size,
        rows * size * width * 2,
    )


def lat_inverse(place, back, table, fields, width, tile, limit):
    everyone, _, lanes = back.shape
    size = table.shape[0]
    merged = fields[0].shape[1]
    strip = pl.BlockSpec((8, merged), lambda n: (n, 0))
    return lat_call(
        functools.partial(lat_inverse_kernel, width=width, count=len(fields)),
        (place, back, table, *fields),
        [
            pl.BlockSpec((everyone, 8, lanes), lambda n: (0, n + tile, 0)),
            pl.BlockSpec((size, size), lambda n: (0, 0)),
        ]
        + [pl.BlockSpec((8, merged), lambda n: (n + tile, 0))] * len(fields),
        [jax.ShapeDtypeStruct((8, merged), jnp.bfloat16)] * len(fields),
        [strip] * len(fields),
        8,
        size,
        8 * size * width * 2,
        limit,
    )


def assemble_kernel(place, *refs, chunks, rows, count):
    pieces, out = refs[:-1], refs[-1]
    length = out.shape[0]
    for n, (start, stop) in enumerate(chunks):
        for m in range(count):
            piece = pieces[n * count + m]
            block = place[0] ^ m
            rest = length - (count - 1) * rows - start

            def fill(piece=piece, block=block, start=start, stop=stop):
                row = pl.multiple_of(block * rows + start, 8)
                out[pl.ds(row, stop - start), :] = piece[...]

            if rest >= stop - start:
                fill()
            else:
                pl.when(block < count - 1)(fill)

                @pl.when(block == count - 1)
                def _(piece=piece, rest=rest):
                    out[pl.ds(length - rest, rest), :] = piece[pl.ds(0, rest), :]


def insert_kernel(place, *refs, start, rows, count):
    pieces, out, sems = refs[:count], refs[-2], refs[-1]
    copies = []
    for m in range(count):
        row = pl.multiple_of((place[0] ^ m) * rows + start, 8)
        copies.append(
            pltpu.make_async_copy(pieces[m], out.at[pl.ds(row, pieces[m].shape[0])], sems.at[m])
        )
        copies[-1].start()
    for copy in copies:
        copy.wait()


def assemble(place, mixed, chunks, rows, length):
    whole, away = pl.BlockSpec(memory_space=pltpu.VMEM), pl.BlockSpec(memory_space=pl.ANY)
    scalar = pl.BlockSpec(memory_space=pltpu.SMEM)
    pieces = [piece for chunk in mixed[:-1] for piece in chunk]
    count = len(mixed[0])
    shape = jax.ShapeDtypeStruct((length, pieces[0].shape[1]), jnp.bfloat16)
    most = pl.pallas_call(
        functools.partial(assemble_kernel, chunks=chunks[:-1], rows=rows, count=count),
        out_shape=shape,
        in_specs=[scalar] + [whole] * len(pieces),
        out_specs=whole,
        compiler_params=pltpu.CompilerParams(vmem_limit_bytes=16 * 2**20),
        cost_estimate=pl.CostEstimate(flops=0, bytes_accessed=5 * 10**6, transcendentals=0),
        name="assemble",
    )(place, *pieces)
    return pl.pallas_call(
        functools.partial(insert_kernel, start=chunks[-1][0], rows=rows, count=count),
        out_shape=shape,
        in_specs=[scalar] + [whole] * count + [away],
        out_specs=away,
        input_output_aliases={1 + count: 0},
        scratch_shapes=[pltpu.SemaphoreType.DMA((count,))],
        compiler_params=pltpu.CompilerParams(vmem_limit_bytes=16 * 2**20),
        cost_estimate=pl.CostEstimate(flops=0, bytes_accessed=2 * 10**6, transcendentals=0),
        name="insert",
    )(place, *mixed[-1], most)


def swap(pieces, count):
    return [pieces[0]] + [
        lax.ppermute(pieces[m], "lat", [(i, i ^ m) for i in range(count)]) for m in range(1, count)
    ]


def layer(grid_field, first_weight, first_bias, second_weight, second_bias):
    lon_n, lat_n = lax.axis_size("lon"), lax.axis_size("lat")
    width = first_weight.shape[2]
    local_lon, _, merged = grid_field.shape
    local_lat = merged // width
    rows = -(-local_lon // (8 * lat_n)) * 8
    lat_size = local_lat * lat_n
    everyone = lat_n * lon_n
    chunks = ((0, 8), (8, rows))
    tables = [lon_tables(lat_n, lon_n, local_lon, rows, c) for c in chunks]
    fwds = [jnp.asarray(t[0]) for t in tables]
    invs = [jnp.asarray(t[1]) for t in tables]
    lat = lat_table(lat_size)
    lat, lat_back = jnp.asarray(lat), jnp.asarray(np.ascontiguousarray(lat.T))
    special = (lax.axis_index("lat") == 0) & (lax.axis_index("lon") == 0)
    w1 = first_layer(first_weight[0], special)
    b1 = jnp.concatenate([first_bias[0].reshape(-1)] * 2)[None]
    w2, b2 = second_layer(second_weight[0], second_bias[0], 128)
    flag = special.astype(jnp.int32).reshape(1)
    me = lax.axis_index("lat")
    place = me.astype(jnp.int32).reshape(1)

    field = grid_field[:, 0]
    padded = jnp.pad(field, ((0, rows * lat_n - local_lon), (0, 0)))
    exchange = lambda x: lax.all_to_all(x, group, split_axis=0, concat_axis=0, tiled=True)
    flat = lambda x: x.reshape(-1, x.shape[-1])

    fields, xs = [], []
    for start, stop in chunks:
        whole = padded if (lat_n - 1) * rows + stop > local_lon else field
        pieces = [
            lax.dynamic_slice(whole, (rows * (me ^ m) + start, 0), (stop - start, merged))
            for m in range(lat_n)
        ]
        fields.append(swap(pieces, lat_n))
        xs.append(lat_forward(place, fields[-1], lat, everyone, width))
    for n in range(2):
        xs[n] = exchange(xs[n])
    last, y = spectral(flag, [flat(x) for x in xs], fwds, invs[1], w1, b1, w2, b2, lat_n)
    outs = [None, last]
    outs[0] = unwind(invs[0], y, lat_n)
    backs = [None, None]
    for n in (1, 0):
        if n == 0:
            outs[0], backs[1] = lax.optimization_barrier((outs[0], backs[1]))
        backs[n] = exchange(outs[n].reshape(everyone, chunks[n][1] - chunks[n][0], -1))
    strips, mixed = [], []
    for n in (1, 0):
        start, stop = chunks[n]
        for first in range(start, stop, 8):
            pieces = lat_inverse(
                place, backs[n], lat_back, fields[n], width, (first - start) // 8, LIMITS[n]
            )
            mixed.append(swap(pieces, lat_n))
            strips.append((first, first + 8))
    return assemble(place, mixed, strips, rows, local_lon)[:, None, :]


def solution(mesh):
    in_specs = (
        P("lon", "ch", "lat"),
        P("ch", None, None, None),
        P("ch", None, None),
        P("ch", None, None, None),
        P("ch", None, None),
    )
    return jax.shard_map(
        layer, mesh=mesh, in_specs=in_specs, out_specs=P("lon", "ch", "lat"), check_vma=False
    )
```

```python
import functools
import math

import jax
import jax.numpy as jnp
import numpy as np
from jax import lax
from jax.experimental import pallas as pl
from jax.experimental.pallas import tpu as pltpu
from jax.sharding import PartitionSpec as P


shrink_level = 0.01
group = ("lat", "lon")
LIMITS = (40, 62)


def phases(left, right, length):
    product = (left[:, None].astype(np.int64) * right[None, :]) % length
    angles = product.astype(np.float32) * np.float32(2.0 * math.pi / length)
    angles = angles.astype(np.float64)
    return np.cos(angles).astype(np.float32), np.sin(angles).astype(np.float32)


def lon_tables(lat_devices, lon_devices, local_lon, rows, chunk):
    length = local_lon * lon_devices
    i, j, r = np.meshgrid(
        np.arange(lat_devices), np.arange(lon_devices // 2), np.arange(*chunk), indexing="ij"
    )
    offset = (i * rows + r).reshape(-1)
    place = (j.reshape(-1) * local_lon + offset).astype(np.int64)
    real = (offset < local_lon).astype(np.float32)
    place = np.where(offset < local_lon, place, 0)
    factor = np.float32(1.0 / math.sqrt(length))
    forward, inverse = [], []
    for parity in range(2):
        modes = np.arange(parity, length // 2, 2)
        cosine, sine = phases(modes, place, length)
        extra = ((0, -len(modes) % 16), (0, 0))
        stack = lambda c, q: np.concatenate([np.pad(c, extra), np.pad(-q, extra)], axis=0)
        weights = np.where(modes == 0, 1.0, 2.0).astype(np.float32)[:, None]
        forward.append(stack(cosine, sine) * factor * real)
        inverse.append((stack(cosine * weights, sine * weights) * factor * real).T)
    return np.stack(forward).astype(jnp.bfloat16), np.stack(inverse).astype(jnp.bfloat16)


def lat_table(length):
    half = length // 2
    cosine, sine = phases(np.arange(half + 1), np.arange(length), length)
    sine[0] = cosine[half]
    table = np.stack([cosine[:half], sine[:half]], axis=1).reshape(length, length)
    return (table * np.float32(1.0 / math.sqrt(length))).astype(jnp.bfloat16)


def first_layer(weight, special, lanes):
    u, v = weight[0], weight[1]
    z = jnp.zeros_like(u)
    rows = lambda *blocks: jnp.concatenate([jnp.concatenate(b, axis=1) for b in blocks], axis=0)
    pair = rows((u, v, u, v), (v, -u, -v, u), (-v, u, -v, u), (u, v, -u, -v))
    single = rows((u, v, z, z), (z, z, u, v), (-v, u, z, z), (z, z, -v, u))
    layers = jnp.stack([jnp.where(special, single, pair), pair])
    width = u.shape[0]
    layers = layers.reshape(2, 4 * width, 2, 2 * width)
    spare = 2 * lanes - 2 * width
    return jnp.pad(layers, ((0, 0), (0, 0), (0, 0), (0, spare))).reshape(2, 4 * width, 4 * lanes)


def second_layer(weight, bias, lanes):
    u, v = weight[0], weight[1]
    width = u.shape[0]
    wide = lambda m: jnp.pad(m, ((0, 0), (0, lanes - width)))
    u, v, m = wide(u), wide(v), wide(-v)
    rows = [jnp.concatenate(r, axis=1) for r in ((u, v), (m, u))]
    matrix = jnp.pad(jnp.concatenate(rows, axis=0), ((0, 2 * (lanes - width)), (0, 0)))
    padded = jnp.pad(bias, ((0, 0), (0, lanes - width))).reshape(-1)
    return matrix, padded[None]


def soft_threshold(v):
    return v - jnp.minimum(jnp.maximum(v, -shrink_level), shrink_level)


def fold(x, blocks):
    half = x.shape[0] // (2 * blocks)
    near, far = [
        jnp.concatenate(
            [x[pl.ds((2 * n + side) * half, half), :].astype(jnp.float32) for n in range(blocks)],
            axis=0,
        )
        for side in range(2)
    ]
    return (near + far).astype(jnp.bfloat16), (near - far).astype(jnp.bfloat16)


def unfold(inv, y, out, blocks):
    count = inv.shape[2]
    even, odd = [
        jnp.dot(inv[p], y[pl.ds(p * count, count), :], preferred_element_type=jnp.float32)
        for p in range(2)
    ]
    near, far = (even + odd).astype(out.dtype), (even - odd).astype(out.dtype)
    half = out.shape[0] // (2 * blocks)
    for n in range(blocks):
        out[pl.ds(2 * n * half, half), :] = near[n * half : (n + 1) * half]
        out[pl.ds((2 * n + 1) * half, half), :] = far[n * half : (n + 1) * half]


def spectral_kernel(flag, *refs, chunks, blocks):
    xs, fwds = refs[:chunks], refs[chunks : 2 * chunks]
    inv, w1, b1, w2, b2, out, y, z = refs[2 * chunks :]
    count = fwds[0].shape[1]
    kept = count // 2
    width = w1.shape[1] // 4
    slots = y.shape[1] // (2 * width)
    lanes = w2.shape[1] // 2
    folded = [fold(x, blocks) for x in xs]
    for p in range(2):
        total = None
        for fwd, pair in zip(fwds, folded):
            term = jnp.dot(fwd[p], pair[p], preferred_element_type=jnp.float32)
            total = term if total is None else total + term
        z[pl.ds(p * count, count), :] = total.astype(z.dtype)
    for base, s in [(p * count, s) for p in range(2) for s in range(slots)]:
        cols = pl.ds(s * 2 * width, 2 * width)
        layer = w1[min(s, 1)]
        hidden = jnp.dot(
            z[pl.ds(base, kept), cols], layer[: 2 * width], preferred_element_type=jnp.float32
        )
        hidden = hidden + jnp.dot(
            z[pl.ds(base + kept, kept), cols], layer[2 * width :], preferred_element_type=jnp.float32
        )
        hidden = jnp.maximum(hidden + b1[...], 0.0).astype(jnp.bfloat16)
        parts = []
        for m in range(2):
            v = hidden[:, 2 * m * lanes : 2 * (m + 1) * lanes]
            v = jnp.dot(v, w2[...], preferred_element_type=jnp.float32) + b2[...]
            v = soft_threshold(v)
            parts += [v[:, :lanes], v[:, lanes:]]
        re, im, re2, im2 = parts
        top = (re + re2, im2 - im)
        bottom = (im + im2, re - re2)
        if s == 0:
            alone = flag[0] == 1
            top = (jnp.where(alone, re, top[0]), jnp.where(alone, re2, top[1]))
            bottom = (jnp.where(alone, im, bottom[0]), jnp.where(alone, im2, bottom[1]))
        for start, (a, b) in ((base, top), (base + kept, bottom)):
            y[pl.ds(start, kept), cols] = jnp.concatenate(
                [a[:, :width], b[:, :width]], axis=1
            ).astype(y.dtype)
    unfold(inv, y, out, blocks)


def unwind_kernel(inv, y, out, *, blocks):
    unfold(inv, y, out, blocks)


def unwind(inv, y, blocks):
    whole = pl.BlockSpec(memory_space=pltpu.VMEM)
    return pl.pallas_call(
        functools.partial(unwind_kernel, blocks=blocks),
        out_shape=jax.ShapeDtypeStruct((2 * inv.shape[1], y.shape[1]), jnp.bfloat16),
        in_specs=[whole] * 2,
        out_specs=whole,
        compiler_params=pltpu.CompilerParams(vmem_limit_bytes=62 * 2**20),
        cost_estimate=pl.CostEstimate(
            flops=10**9, bytes_accessed=4 * 10**6, transcendentals=0
        ),
        name="unwind",
    )(inv, y)


def spectral(flag, xs, fwds, inv, w1, b1, w2, b2, blocks):
    whole = pl.BlockSpec(memory_space=pltpu.VMEM)
    rows, cols = 2 * fwds[0].shape[1], xs[0].shape[1]
    return pl.pallas_call(
        functools.partial(spectral_kernel, chunks=len(xs), blocks=blocks),
        out_shape=[
            jax.ShapeDtypeStruct((2 * inv.shape[1], cols), jnp.bfloat16),
            jax.ShapeDtypeStruct((rows, cols), jnp.bfloat16),
        ],
        in_specs=[pl.BlockSpec(memory_space=pltpu.SMEM)] + [whole] * (2 * len(xs) + 5),
        out_specs=[whole, whole],
        scratch_shapes=[pltpu.VMEM((rows, cols), jnp.bfloat16)],
        compiler_params=pltpu.CompilerParams(vmem_limit_bytes=60 * 2**20),
        cost_estimate=pl.CostEstimate(
            flops=9 * 10**9, bytes_accessed=14 * 10**6, transcendentals=0
        ),
        name="spectral",
    )(flag, *xs, *fwds, inv, w1, b1, w2, b2)


def spread(scratch, start, group, width):
    for n in range(group.shape[1] // width):
        scratch[pl.ds(start + 8 * n, 8), pl.ds(0, width)] = group[:, n * width : (n + 1) * width]


def gather(scratch, start, count, width):
    return jnp.concatenate(
        [scratch[pl.ds(start + 8 * n, 8), :][:, :width] for n in range(count)], axis=1
    )


def transform(table, source, target, size):
    for r in range(0, 8, 2):
        pair = [source[pl.ds(r + k, size, stride=8), :].astype(jnp.bfloat16) for k in range(2)]
        sums = jnp.dot(
            table[...], jnp.concatenate(pair, axis=1), preferred_element_type=jnp.float32
        )
        for k in range(2):
            target[pl.ds(r + k, size, stride=8), :] = sums[:, k * 128 : (k + 1) * 128]


def lat_forward_kernel(place, *refs, width):
    fields, (table, out, source, target) = refs[:-4], refs[-4:]
    size = table.shape[0]
    span = 4 * width
    local = size // len(fields)
    bases = [(place[0] ^ m) * (8 * local) for m in range(len(fields))]

    def step(g, carry):
        lanes = pl.ds(pl.multiple_of(g * span, 128), span)
        for field, base in zip(fields, bases):
            start = pl.multiple_of(base + g * 32, 8)
            spread(source, start, field[:, lanes].astype(jnp.float32), width)
        return carry

    lax.fori_loop(0, local // 4, step, 0, unroll=8)
    transform(table, source, target, size)
    per = out.shape[2] // span

    def finish(d, carry):
        for p in range(per):
            start = pl.multiple_of((d * per + p) * 32, 8)
            out[d, :, pl.ds(p * span, span)] = gather(target, start, 4, width).astype(out.dtype)
        return carry

    lax.fori_loop(0, out.shape[0], finish, 0, unroll=16)


def lat_inverse_kernel(place, back, table, *refs, width, count):
    fields, outs, (source, target) = refs[:count], refs[count : 2 * count], refs[2 * count :]
    size = table.shape[0]
    span = 4 * width
    local = size // count
    per = back.shape[2] // span

    def begin(d, carry):
        for p in range(per):
            start = pl.multiple_of((d * per + p) * 32, 8)
            spread(source, start, back[d, :, pl.ds(p * span, span)].astype(jnp.float32), width)
        return carry

    lax.fori_loop(0, back.shape[0], begin, 0, unroll=16)
    transform(table, source, target, size)
    bases = [(place[0] ^ m) * (8 * local) for m in range(count)]

    def step(g, carry):
        lanes = pl.ds(pl.multiple_of(g * span, 128), span)
        for field, out, base in zip(fields, outs, bases):
            sums = gather(target, pl.multiple_of(base + g * 32, 8), 4, width)
            out[:, lanes] = (sums + field[:, lanes].astype(jnp.float32)).astype(out.dtype)
        return carry

    lax.fori_loop(0, local // 4, step, 0, unroll=8)


def lat_call(kernel, args, in_specs, out_shape, out_specs, rows, size, moved, limit=40):
    return pl.pallas_call(
        kernel,
        grid=(rows // 8,),
        out_shape=out_shape,
        in_specs=[pl.BlockSpec(memory_space=pltpu.SMEM)] + in_specs,
        out_specs=out_specs,
        scratch_shapes=[pltpu.VMEM((8 * size, 128), jnp.float32)] * 2,
        compiler_params=pltpu.CompilerParams(vmem_limit_bytes=limit * 2**20),
        cost_estimate=pl.CostEstimate(
            flops=2 * rows * size * size * 128, bytes_accessed=2 * moved, transcendentals=0
        ),
    )(*args)


def lat_forward(place, fields, table, everyone, width):
    rows, merged = fields[0].shape
    size = table.shape[0]
    lanes = size * width // everyone
    strip = pl.BlockSpec((8, merged), lambda n: (n, 0))
    return lat_call(
        functools.partial(lat_forward_kernel, width=width),
        (place, *fields, table),
        [strip] * len(fields) + [pl.BlockSpec((size, size), lambda n: (0, 0))],
        jax.ShapeDtypeStruct((everyone, rows, lanes), jnp.bfloat16),
        pl.BlockSpec((everyone, 8, lanes), lambda n: (0, n, 0)),
        rows,
        size,
        rows * size * width * 2,
    )


def lat_inverse(place, back, table, fields, width, tile, limit):
    everyone, _, lanes = back.shape
    size = table.shape[0]
    merged = fields[0].shape[1]
    strip = pl.BlockSpec((8, merged), lambda n: (n, 0))
    return lat_call(
        functools.partial(lat_inverse_kernel, width=width, count=len(fields)),
        (place, back, table, *fields),
        [
            pl.BlockSpec((everyone, 8, lanes), lambda n: (0, n + tile, 0)),
            pl.BlockSpec((size, size), lambda n: (0, 0)),
        ]
        + [pl.BlockSpec((8, merged), lambda n: (n + tile, 0))] * len(fields),
        [jax.ShapeDtypeStruct((8, merged), jnp.bfloat16)] * len(fields),
        [strip] * len(fields),
        8,
        size,
        8 * size * width * 2,
        limit,
    )


def assemble_kernel(place, *refs, chunks, rows, count):
    pieces, out = refs[:-1], refs[-1]
    length = out.shape[0]
    for n, (start, stop) in enumerate(chunks):
        for m in range(count):
            piece = pieces[n * count + m]
            block = place[0] ^ m
            rest = length - (count - 1) * rows - start

            def fill(piece=piece, block=block, start=start, stop=stop):
                row = pl.multiple_of(block * rows + start, 8)
                out[pl.ds(row, stop - start), :] = piece[...]

            if rest >= stop - start:
                fill()
            else:
                pl.when(block < count - 1)(fill)

                @pl.when(block == count - 1)
                def _(piece=piece, rest=rest):
                    out[pl.ds(length - rest, rest), :] = piece[pl.ds(0, rest), :]


def insert_kernel(place, *refs, start, rows, count):
    pieces, out, sems = refs[:count], refs[-2], refs[-1]
    copies = []
    for m in range(count):
        row = pl.multiple_of((place[0] ^ m) * rows + start, 8)
        copies.append(
            pltpu.make_async_copy(pieces[m], out.at[pl.ds(row, pieces[m].shape[0])], sems.at[m])
        )
        copies[-1].start()
    for copy in copies:
        copy.wait()


def assemble(place, mixed, chunks, rows, length):
    whole, away = pl.BlockSpec(memory_space=pltpu.VMEM), pl.BlockSpec(memory_space=pl.ANY)
    scalar = pl.BlockSpec(memory_space=pltpu.SMEM)
    pieces = [piece for chunk in mixed[:-1] for piece in chunk]
    count = len(mixed[0])
    shape = jax.ShapeDtypeStruct((length, pieces[0].shape[1]), jnp.bfloat16)
    most = pl.pallas_call(
        functools.partial(assemble_kernel, chunks=chunks[:-1], rows=rows, count=count),
        out_shape=shape,
        in_specs=[scalar] + [whole] * len(pieces),
        out_specs=whole,
        compiler_params=pltpu.CompilerParams(vmem_limit_bytes=16 * 2**20),
        cost_estimate=pl.CostEstimate(flops=0, bytes_accessed=5 * 10**6, transcendentals=0),
        name="assemble",
    )(place, *pieces)
    return pl.pallas_call(
        functools.partial(insert_kernel, start=chunks[-1][0], rows=rows, count=count),
        out_shape=shape,
        in_specs=[scalar] + [whole] * count + [away],
        out_specs=away,
        input_output_aliases={1 + count: 0},
        scratch_shapes=[pltpu.SemaphoreType.DMA((count,))],
        compiler_params=pltpu.CompilerParams(vmem_limit_bytes=16 * 2**20),
        cost_estimate=pl.CostEstimate(flops=0, bytes_accessed=2 * 10**6, transcendentals=0),
        name="insert",
    )(place, *mixed[-1], most)


def swap(pieces, count):
    return [pieces[0]] + [
        lax.ppermute(pieces[m], "lat", [(i, i ^ m) for i in range(count)]) for m in range(1, count)
    ]


def layer(grid_field, first_weight, first_bias, second_weight, second_bias):
    lon_n, lat_n = lax.axis_size("lon"), lax.axis_size("lat")
    width = first_weight.shape[2]
    local_lon, _, merged = grid_field.shape
    local_lat = merged // width
    rows = -(-local_lon // (8 * lat_n)) * 8
    lat_size = local_lat * lat_n
    everyone = lat_n * lon_n
    chunks = ((0, 8), (8, rows))
    tables = [lon_tables(lat_n, lon_n, local_lon, rows, c) for c in chunks]
    fwds = [jnp.asarray(t[0]) for t in tables]
    invs = [jnp.asarray(t[1]) for t in tables]
    lat = lat_table(lat_size)
    lat, lat_back = jnp.asarray(lat), jnp.asarray(np.ascontiguousarray(lat.T))
    special = (lax.axis_index("lat") == 0) & (lax.axis_index("lon") == 0)
    w1 = first_layer(first_weight[0], special, 128)
    b1 = jnp.pad(first_bias[0].reshape(-1), (0, 256 - 2 * width))
    b1 = jnp.concatenate([b1, b1])[None]
    w2, b2 = second_layer(second_weight[0], second_bias[0], 128)
    flag = special.astype(jnp.int32).reshape(1)
    me = lax.axis_index("lat")
    place = me.astype(jnp.int32).reshape(1)

    field = grid_field[:, 0]
    padded = jnp.pad(field, ((0, rows * lat_n - local_lon), (0, 0)))
    exchange = lambda x: lax.all_to_all(x, group, split_axis=0, concat_axis=0, tiled=True)
    flat = lambda x: x.reshape(-1, x.shape[-1])

    fields, xs = [], []
    for start, stop in chunks:
        whole = padded if (lat_n - 1) * rows + stop > local_lon else field
        pieces = [
            lax.dynamic_slice(whole, (rows * (me ^ m) + start, 0), (stop - start, merged))
            for m in range(lat_n)
        ]
        fields.append(swap(pieces, lat_n))
        xs.append(lat_forward(place, fields[-1], lat, everyone, width))
    for n in range(2):
        xs[n] = exchange(xs[n])
    last, y = spectral(flag, [flat(x) for x in xs], fwds, invs[1], w1, b1, w2, b2, lat_n)
    outs = [None, last]
    outs[0] = unwind(invs[0], y, lat_n)
    backs = [None, None]
    for n in (1, 0):
        if n == 0:
            outs[0], backs[1] = lax.optimization_barrier((outs[0], backs[1]))
        backs[n] = exchange(outs[n].reshape(everyone, chunks[n][1] - chunks[n][0], -1))
    strips, mixed = [], []
    for n in (1, 0):
        start, stop = chunks[n]
        for first in range(start, stop, 8):
            pieces = lat_inverse(
                place, backs[n], lat_back, fields[n], width, (first - start) // 8, LIMITS[n]
            )
            mixed.append(swap(pieces, lat_n))
            strips.append((first, first + 8))
    return assemble(place, mixed, strips, rows, local_lon)[:, None, :]


def solution(mesh):
    in_specs = (
        P("lon", "ch", "lat"),
        P("ch", None, None, None),
        P("ch", None, None),
        P("ch", None, None, None),
        P("ch", None, None),
    )
    return jax.shard_map(
        layer, mesh=mesh, in_specs=in_specs, out_specs=P("lon", "ch", "lat"), check_vma=False
    )
```
